32 devices in a mesh: groups: 2 (over x), queue: 16 (over z, y, core).
Axes of the slice: x: 2, y: 2, z: 4, core: 2. Of those that a mesh axis runs over, the one named last changes fastest.
Arguments:
- hidden: bfloat16 [256, 5120], P(('groups', 'queue')), parts along dimension 0, may hold values from -6 to 6
- incoming: bfloat16 [2, 16, 5120], P(None, 'groups'), parts along dimension 1, may hold values from -6 to 6
- levels: int32 [16], replicated, may hold values from 0 to 95, as said below
- mod_table: bfloat16 [96, 3, 5120], replicated, may hold values from -3 to 3
- query_weight: bfloat16 [5120, 5120], P(None, 'queue'), may hold values from -0.078125 to 0.078125
- key_weight: bfloat16 [5120, 5120], P(None, 'queue'), may hold values from -0.078125 to 0.078125
- value_weight: bfloat16 [5120, 5120], P(None, 'queue'), may hold values from -0.078125 to 0.078125
- output_weight: bfloat16 [5120, 5120], P(None, 'queue'), may hold values from -0.078125 to 0.078125
- query_gain: float32 [5120], replicated, may hold values from 0.5 to 1.5
- key_gain: float32 [5120], replicated, may hold values from 0.5 to 1.5
- text_keys: bfloat16 [1024, 5120], P(('groups', 'queue')), parts along dimension 0, may hold values from -6 to 6
- text_values: bfloat16 [1024, 5120], P(('groups', 'queue')), parts along dimension 0, may hold values from -6 to 6
Outputs:
- updated: bfloat16 [256, 5120], P(('groups', 'queue')), parts along dimension 0
The draws below stay inside these ranges and needn't reach their ends.
There are 2 independent parts, one for each index of `groups`. The reference program is written for one: setup_inputs(seed, part) draws one part's arguments, and reference() takes and returns one part's arrays. A program takes and returns all parts, laid end to end along the dimension named above; an argument that names none is the same for every part. Nothing has to cross between parts.
Inputs may be any that keep to these rules, and one draw needn't show every extreme that they name: `levels`: strictly rising along the queue positions; the last position always has level 95.
All inputs are finite; a program needn't handle non-finite values.
Results may differ from the reference program's by a relative error of at most 0.0085.
Values may be sent and summed in bfloat16 or wider, within the bound.
A program may use at most 128 MiB of HBM per device.

```python
import math
import jax
import jax.numpy as jnp
from jax import lax

D = 5120
HEADS = 40
HD = 128
TOK_DEV = 8
STEPS = 2
LEVELS = 96
TEXT = 512
SPANS = 16
TOKENS = 128


def draw_levels(key, part):
    order = jax.random.permutation(key, LEVELS - 1)
    picked = jnp.sort(order[:SPANS - 1])
    return jnp.concatenate([picked, jnp.array([LEVELS - 1])]).astype(jnp.int32)


def block_levels(own_key, extent, cuts, low, top_value):
    gain = 1.0
    for dim, parts in cuts:
        heights = jax.random.uniform(jax.random.fold_in(jax.random.fold_in(own_key, 6), dim), (parts,), jnp.float32, low / len(cuts), top_value / len(cuts))
        gain = gain * jnp.repeat(jnp.exp(heights), extent[dim] // parts).reshape((-1,) + (1,) * (len(extent) - 1 - dim))
    return gain


def normal_values(key, extent, deviation, most, cuts=(), held_as=jnp.bfloat16):
    drawn = jax.random.normal(key, extent, jnp.float32) * deviation
    if len(cuts) > 0:
        drawn = block_levels(key, extent, cuts, -0.22, 0.18) * drawn
    return jnp.clip(drawn, min=-most, max=most).astype(held_as)


def setup_inputs(seed: int = 0, part: int = 0) -> dict:
    key_list = jax.random.split(jax.random.key(seed), 13)
    part_splits = jax.random.split(jax.random.fold_in(key_list[12], part), 13)
    return {
        "hidden": normal_values(part_splits[0], (TOKENS, D), 1.0, 6.0, ((0, 16),)),
        "incoming": normal_values(part_splits[1], (STEPS, TOK_DEV, D), 1.0, 6.0),
        "levels": draw_levels(jax.random.fold_in(key_list[12], 71), part),
        "mod_table": normal_values(key_list[3], (LEVELS, 3, D), 0.5, 3.0),
        "query_weight": normal_values(key_list[4], (D, D), D ** -0.5, 0.078125, ((1, 16),)),
        "key_weight": normal_values(key_list[5], (D, D), D ** -0.5, 0.078125, ((1, 16),)),
        "value_weight": normal_values(key_list[6], (D, D), D ** -0.5, 0.078125, ((1, 16),)),
        "output_weight": normal_values(key_list[7], (D, D), D ** -0.5, 0.078125, ((1, 16),)),
        "query_gain": jnp.clip(1.0 + 0.1 * jax.random.normal(key_list[8], (D,), jnp.float32), 0.5, 1.5),
        "key_gain": jnp.clip(1.0 + 0.1 * jax.random.normal(key_list[9], (D,), jnp.float32), 0.5, 1.5),
        "text_keys": normal_values(part_splits[10], (TEXT, D), 1.0, 6.0, ((0, 16),)),
        "text_values": normal_values(part_splits[11], (TEXT, D), 1.0, 6.0, ((0, 16),)),
    }


def normalize(values):
    return values * lax.rsqrt(lax.optimization_barrier(jnp.mean(values * values, axis=-1, keepdims=True)) + 1e-06)

def softmax_rounded(scores):
    row_max = lax.optimization_barrier(jnp.max(scores, axis=-1, keepdims=True))
    weights = jnp.exp(scores - row_max)
    return (weights / lax.optimization_barrier(jnp.sum(weights, axis=-1, keepdims=True))).astype(jnp.bfloat16)

def reference(hidden, incoming, levels, mod_table, query_weight, key_weight, value_weight, output_weight, query_gain, key_gain, text_keys, text_values):
    modulation = jnp.take(mod_table, levels.astype(jnp.int32), axis=0).astype(jnp.float32)[:, None]
    score_scale = 1.0 / math.sqrt(HD)
    total_rows = SPANS * TOK_DEV
    span_of = (jnp.arange(total_rows) // TOK_DEV).astype(jnp.int32)
    allowed = span_of[:, None] >= span_of[None, :]
    text_k = text_keys.reshape(TEXT, HEADS, HD).transpose(1, 0, 2)
    text_v = text_values.reshape(TEXT, HEADS, HD).transpose(1, 0, 2)

    def one_head(operands):
        q_one, k_one, v_one, tk_one, tv_one = operands
        scores = jnp.dot(q_one, k_one.T, preferred_element_type=jnp.float32) * score_scale
        scores = jnp.where(allowed, scores, -1e+30)
        attended = jnp.dot(softmax_rounded(scores), v_one, preferred_element_type=jnp.float32).astype(jnp.bfloat16)
        text_scores = jnp.dot(q_one, tk_one.T, preferred_element_type=jnp.float32) * score_scale
        crossed = jnp.dot(softmax_rounded(text_scores), tv_one, preferred_element_type=jnp.float32).astype(jnp.bfloat16)
        return (attended.astype(jnp.float32) + crossed.astype(jnp.float32)).astype(jnp.bfloat16)
    queue_state = hidden
    for section_index in range(STEPS):
        queue_state = jnp.concatenate([incoming[section_index], queue_state[:-TOK_DEV]], axis=0)
        current = queue_state.astype(jnp.float32).reshape(SPANS, TOK_DEV, D)
        modulated = (normalize(current) * (1.0 + modulation[:, :, 1]) + modulation[:, :, 0]).astype(jnp.bfloat16)
        modulated = modulated.reshape(total_rows, D)
        query_rows = (normalize(jnp.dot(modulated, query_weight, preferred_element_type=jnp.float32)) * query_gain).astype(jnp.bfloat16)
        key_rows = (normalize(jnp.dot(modulated, key_weight, preferred_element_type=jnp.float32)) * key_gain).astype(jnp.bfloat16)
        value_rows = jnp.dot(modulated, value_weight, preferred_element_type=jnp.float32).astype(jnp.bfloat16)
        query_heads = query_rows.reshape(total_rows, HEADS, HD).transpose(1, 0, 2)
        key_heads = key_rows.reshape(total_rows, HEADS, HD).transpose(1, 0, 2)
        value_heads = value_rows.reshape(total_rows, HEADS, HD).transpose(1, 0, 2)
        combined = lax.map(one_head, (query_heads, key_heads, value_heads, text_k, text_v))
        combined = combined.transpose(1, 0, 2).reshape(total_rows, D)
        projected = jnp.dot(combined, output_weight, preferred_element_type=jnp.float32).reshape(SPANS, TOK_DEV, D)
        queue_state = (current + modulation[:, :, 2] * projected).astype(jnp.bfloat16).reshape(total_rows, D)
    return queue_state
```

```python
import functools
import math

import jax
import jax.numpy as jnp
from jax import lax
from jax.experimental import pallas as pl
from jax.experimental.pallas import tpu as pltpu
from jax.sharding import PartitionSpec as P

HEADS = 40
STEPS = 2


def passed_along(value, axis, steps):
    count = lax.axis_size(axis)
    initial, last = (max(0, -steps), min(count, count - steps))
    return lax.ppermute(value, axis, [(source, source + steps) for source in range(initial, last)])


def normalize(values):
    return values * lax.rsqrt(jnp.mean(values * values, axis=-1, keepdims=True) + 1e-06)


def softmax_rounded(scores):
    row_max = jnp.max(scores, axis=-1, keepdims=True)
    weights = jnp.exp(scores - row_max)
    return (weights / jnp.sum(weights, axis=-1, keepdims=True)).astype(jnp.bfloat16)


def pad_slots(values, slot_total):
    missing = slot_total - values.shape[1]
    filler = jnp.zeros((values.shape[0], missing, values.shape[2]), values.dtype)
    return jnp.concatenate([values, filler], axis=1)


def causal_block(queries, keys_all, values_all, span_rows, score_scale):
    total_rows = queries.shape[0]
    block_rows = min(512, total_rows)
    scores = (
        jnp.einsum("qsd,ksd->sqk", queries, keys_all, preferred_element_type=jnp.float32)
        * score_scale
    )
    allowed = (
        jnp.arange(0, block_rows)[:, None] // span_rows
        >= jnp.arange(block_rows)[None, :] // span_rows
    )
    scores = jnp.where(allowed[None], scores, -1e30)
    result = jnp.einsum(
        "sqk,ksd->qsd", softmax_rounded(scores), values_all, preferred_element_type=jnp.float32
    )
    pieces = result.astype(jnp.bfloat16)
    return pieces


def text_attend(queries, text_k, text_v, score_scale):
    scores = (
        jnp.einsum("qsd,tsd->sqt", queries, text_k, preferred_element_type=jnp.float32)
        * score_scale
    )
    return jnp.einsum(
        "sqt,tsd->qsd", softmax_rounded(scores), text_v, preferred_element_type=jnp.float32
    ).astype(jnp.bfloat16)


def per_device(
    hidden,
    incoming,
    levels,
    mod_table,
    query_weight,
    key_weight,
    value_weight,
    output_weight,
    query_gain,
    key_gain,
    text_keys,
    text_values,
):
    own_index = lax.axis_index("queue")
    queue_size = lax.axis_size("queue")
    span_rows, model_width = hidden.shape
    head_size = model_width // HEADS
    score_scale = 1.0 / math.sqrt(head_size)
    slot_total = -(-HEADS // queue_size) * queue_size
    own_level = lax.dynamic_index_in_dim(levels, own_index, 0, keepdims=False)
    modulation = lax.dynamic_index_in_dim(mod_table, own_level, 0, keepdims=False).astype(
        jnp.float32
    )
    stacked_weights = jnp.stack([query_weight, key_weight, value_weight])
    text_local = text_keys.shape[0]
    text_k_slots, text_v_slots = (
        lax.all_to_all(
            pad_slots(text_keys.reshape(text_local, HEADS, head_size), slot_total),
            "queue",
            split_axis=1,
            concat_axis=0,
            tiled=True,
        ),
        lax.all_to_all(
            pad_slots(text_values.reshape(text_local, HEADS, head_size), slot_total),
            "queue",
            split_axis=1,
            concat_axis=0,
            tiled=True,
        ),
    )
    queue_state = hidden
    for section_index in range(STEPS):
        shifted = passed_along(queue_state, "queue", 1)
        queue_state = jnp.where(own_index == 0, incoming[section_index], shifted)
        current = queue_state.astype(jnp.float32)
        modulated = (normalize(current) * (1.0 + modulation[1]) + modulation[0]).astype(
            jnp.bfloat16
        )
        columns = jnp.einsum(
            "rd,cdw->crw",
            lax.all_gather(modulated, "queue", axis=0, tiled=True),
            stacked_weights,
            preferred_element_type=jnp.float32,
        )
        own_rows = lax.all_to_all(
            columns.astype(jnp.bfloat16), "queue", split_axis=1, concat_axis=2, tiled=True
        ).astype(columns.dtype)
        query_heads = (
            (normalize(own_rows[0]) * query_gain)
            .astype(jnp.bfloat16)
            .reshape(span_rows, HEADS, head_size)
        )
        key_heads = (
            (normalize(own_rows[1]) * key_gain)
            .astype(jnp.bfloat16)
            .reshape(span_rows, HEADS, head_size)
        )
        value_heads = own_rows[2].astype(jnp.bfloat16).reshape(span_rows, HEADS, head_size)
        query_slots, key_slots, value_slots = (
            lax.all_to_all(
                pad_slots(query_heads, slot_total), "queue", split_axis=1, concat_axis=0, tiled=True
            ),
            lax.all_to_all(
                pad_slots(key_heads, slot_total), "queue", split_axis=1, concat_axis=0, tiled=True
            ),
            lax.all_to_all(
                pad_slots(value_heads, slot_total), "queue", split_axis=1, concat_axis=0, tiled=True
            ),
        )
        attended_slots = causal_block(query_slots, key_slots, value_slots, span_rows, score_scale)
        crossed_slots = text_attend(query_slots, text_k_slots, text_v_slots, score_scale)
        attended_back, crossed_back = (
            lax.all_to_all(attended_slots, "queue", split_axis=0, concat_axis=1, tiled=True),
            lax.all_to_all(crossed_slots, "queue", split_axis=0, concat_axis=1, tiled=True),
        )
        attended = attended_back[:, :HEADS]
        crossed = crossed_back[:, :HEADS]
        combined = (
            (attended.astype(jnp.float32) + crossed.astype(jnp.float32))
            .astype(jnp.bfloat16)
            .reshape(span_rows, model_width)
        )
        out_columns = jnp.dot(
            lax.all_gather(combined, "queue", axis=0, tiled=True),
            output_weight,
            preferred_element_type=jnp.float32,
        )
        projected = lax.all_to_all(
            out_columns.astype(jnp.bfloat16), "queue", split_axis=0, concat_axis=1, tiled=True
        ).astype(out_columns.dtype)
        queue_state = (current + modulation[2] * projected).astype(jnp.bfloat16)
    return queue_state


def dot_nt(a, b):
    return lax.dot_general(a, b, (((1,), (1,)), ((), ())), preferred_element_type=jnp.float32)


def fused_kernel(
    n,
    cols,
    hidden,
    incoming,
    mods,
    wq_hbm,
    wk_hbm,
    wv_hbm,
    wo_hbm,
    q_gain,
    k_gain,
    tkeys,
    tvals,
    out,
    wq,
    wk,
    wv,
    wo,
    first,
    gathered,
    current,
    full,
    placed,
    qb,
    kb,
    vb,
    xsend,
    xrecv,
    ssend,
    srecv,
    tk,
    tv,
    osend,
    orecv,
    load_sems,
    gsend_sems,
    grecv_sems,
    ssend_sems,
    srecv_sems,
    xsend_sems,
    xrecv_sems,
    tsend_sems,
    trecv_sems,
    osend_sems,
    orecv_sems,
):
    me = lax.axis_index("queue")
    span, width = hidden.shape
    head = width // HEADS
    rows = n * span
    pair = 2 * cols
    local = placed.shape[1]
    shared = 2 * local - pair
    step_off = pair - local
    core = lax.rem(me, 2)
    sibling = me + 1 - 2 * core
    across = me + 2 - 4 * lax.rem(me // 2, 2)
    outer = n // 4
    start_col = pl.multiple_of((me // 2) * pair + core * step_off, 128)
    mid = pl.multiple_of((1 - core) * step_off, 128)
    trows = tkeys.shape[0]
    scale = 1.0 / math.sqrt(head)

    loads = [
        pltpu.make_async_copy(s, d, load_sems.at[i])
        for i, (s, d) in enumerate(((wq_hbm, wq), (wk_hbm, wk), (wv_hbm, wv), (wo_hbm, wo)))
    ]
    own = pltpu.make_async_copy(hidden, first.at[me], load_sems.at[4])
    own.start()
    own_tk = pltpu.make_async_copy(
        tkeys.at[:, pl.ds(start_col, local)], tk.at[pl.ds(me * trows, trows)], load_sems.at[5]
    )
    own_tv = pltpu.make_async_copy(
        tvals.at[:, pl.ds(start_col, local)], tv.at[pl.ds(me * trows, trows)], load_sems.at[6]
    )
    for item in loads + [own_tk, own_tv]:
        item.start()

    barrier = pltpu.get_barrier_semaphore()
    for k in range(1, n):
        pl.semaphore_signal(
            barrier,
            inc=1,
            device_id={"queue": lax.rem(me + k, n)},
            device_id_type=pl.DeviceIdType.MESH,
        )
    pl.semaphore_wait(barrier, n - 1)

    pending = []

    def remote(src, dst, send, recv, target):
        return pltpu.make_async_remote_copy(
            src_ref=src,
            dst_ref=dst,
            send_sem=send,
            recv_sem=recv,
            device_id={"queue": target},
            device_id_type=pl.DeviceIdType.MESH,
        )

    def gather(buf, phase):
        count = [0]

        def push(slot, target):
            i = count[0]
            count[0] += 1
            c = remote(
                buf.at[slot],
                buf.at[slot],
                gsend_sems.at[phase, i],
                grecv_sems.at[phase, slot],
                target,
            )
            c.start()
            pending.append(c)

        def arrived(slot):
            remote(
                buf.at[slot],
                buf.at[slot],
                gsend_sems.at[phase, 0],
                grecv_sems.at[phase, slot],
                sibling,
            ).wait_recv()

        order = sorted(range(1, outer), key=lambda d: min(d, outer - d))
        for d in order:
            push(me, lax.rem(me + 4 * d, n))
        push(me, across)
        push(me, sibling)
        for d in order:
            slot = lax.rem(me + n - 4 * d, n)
            arrived(slot)
            push(slot, across)
            push(slot, sibling)
        for d in [0] + order:
            slot = lax.rem(across + n - 4 * d, n)
            arrived(slot)
            push(slot, sibling)
        for d in [0] + order:
            arrived(lax.rem(sibling + n - 4 * d, n))
        for d in [0] + order:
            base = me + 3 - 2 * lax.rem(me, 4)
            arrived(lax.rem(base + n - 4 * d, n))

    def drain():
        for c in pending:
            c.wait_send()
        pending.clear()

    lane = lax.broadcasted_iota(jnp.int32, (rows, local), 1)
    shift = core * (local - cols)
    mine = (lane >= shift) & (lane < shift + cols)

    def place(value):
        placed[:, :cols] = value
        placed[:, cols:] = jnp.zeros((rows, local - cols), jnp.float32)
        y = placed[...]
        return jnp.where(mine, jnp.where(core == 1, pltpu.roll(y, local - cols, 1), y), 0.0)

    def assemble(buf, dst, base, count):
        for p in range(n // 2):
            a = buf[2 * p, :count]
            b = buf[2 * p + 1, :count]
            at = p * pair
            kept = pl.ds(base, count)
            dst[kept, at : at + step_off] = a[:, :step_off].astype(dst.dtype)
            dst[kept, at + step_off : at + local] = (
                a[:, step_off:].astype(jnp.float32) + b[:, :shared].astype(jnp.float32)
            ).astype(dst.dtype)
            dst[kept, at + local : at + pair] = b[:, shared:].astype(dst.dtype)

    def modulate():
        def body(i, carry):
            r0 = pl.multiple_of(i * 2 * span, 2 * span)
            c = current[pl.ds(r0, 2 * span), :]
            c = c * lax.rsqrt(jnp.mean(c * c, axis=-1, keepdims=True) + 1e-06)

            def rows_of(kind):
                return jnp.concatenate(
                    [
                        jnp.broadcast_to(mods[kind, pl.ds(2 * i + e, 1), :], (span, width))
                        for e in range(2)
                    ],
                    axis=0,
                )

            full[pl.ds(r0, 2 * span), :] = (c * (1.0 + rows_of(1)) + rows_of(0)).astype(
                jnp.bfloat16
            )
            return carry

        lax.fori_loop(0, n // 2, body, 0)

    qg = q_gain[:, pl.ds(start_col, local)]
    kg = k_gain[:, pl.ds(start_col, local)]
    ones = jnp.ones((8, local), jnp.float32)
    allowed = (
        lax.broadcasted_iota(jnp.int32, (rows, rows), 0) // span
        >= lax.broadcasted_iota(jnp.int32, (rows, rows), 1) // span
    )

    own.wait()
    gather(first, 0)
    text = []
    for k in range(1, n):
        target = lax.rem(me + k, n)
        col = pl.multiple_of((target // 2) * pair + lax.rem(target, 2) * step_off, 128)
        for kind, (s, d) in enumerate(((tkeys, tk), (tvals, tv))):
            c = remote(
                s.at[:, pl.ds(col, local)],
                d.at[pl.ds(me * trows, trows)],
                tsend_sems.at[kind, k],
                trecv_sems.at[kind, me],
                target,
            )
            c.start()
            text.append(c)

    for step in range(STEPS):
        current[0:span, :] = incoming[step].astype(jnp.float32)
        if step == 0:
            for s in range(1, n):
                current[s * span : (s + 1) * span, :] = first[s - 1].astype(jnp.float32)
        else:
            assemble(gathered.at[2 * step - 1], current, span, rows - span)
        modulate()
        if step == 0:
            loads[0].wait()
            loads[1].wait()
        m = full[...]
        q = place(jnp.dot(m, wq[...], preferred_element_type=jnp.float32))
        ssend[step, 0] = dot_nt(ones, q * q)
        qb[...] = (q * qg).astype(jnp.bfloat16)
        k_ = place(jnp.dot(m, wk[...], preferred_element_type=jnp.float32))
        ssend[step, 1] = dot_nt(ones, k_ * k_)
        kb[...] = (k_ * kg).astype(jnp.bfloat16)
        for k in range(1, n):
            c = remote(
                ssend.at[step],
                srecv.at[step, me],
                ssend_sems.at[step, k],
                srecv_sems.at[step, me],
                lax.rem(me + k, n),
            )
            c.start()
            pending.append(c)
        srecv[step, me] = ssend[step]
        xsend[step, 0] = qb[:, pl.ds(mid, shared)]
        xsend[step, 1] = kb[:, pl.ds(mid, shared)]
        swap = remote(
            xsend.at[step], xrecv.at[step], xsend_sems.at[step], xrecv_sems.at[step], sibling
        )
        swap.start()
        if step == 0:
            loads[2].wait()
        vb[...] = place(jnp.dot(m, wv[...], preferred_element_type=jnp.float32)).astype(
            jnp.bfloat16
        )
        swap.wait()
        qb[:, pl.ds(mid, shared)] = qb[:, pl.ds(mid, shared)] + xrecv[step, 0]
        kb[:, pl.ds(mid, shared)] = kb[:, pl.ds(mid, shared)] + xrecv[step, 1]
        for k in range(1, n):
            src = lax.rem(me + k, n)
            remote(
                ssend.at[step],
                srecv.at[step, src],
                ssend_sems.at[step, k],
                srecv_sems.at[step, src],
                sibling,
            ).wait_recv()
        total = jnp.sum(srecv[step], axis=0)
        inv = lax.rsqrt(total * (1.0 / width) + 1e-06)
        q_col = jnp.transpose(jnp.broadcast_to(inv[0, 0:1], (128, rows)))[:, 0:1] * scale
        k_row = inv[1, 0:1]
        if step == 0:
            own_tk.wait()
            own_tv.wait()
            for k in range(1, n):
                src = lax.rem(me + k, n)
                for kind, d in enumerate((tk, tv)):
                    remote(
                        d.at[pl.ds(src * trows, trows)],
                        d.at[pl.ds(src * trows, trows)],
                        tsend_sems.at[kind, k],
                        trecv_sems.at[kind, src],
                        sibling,
                    ).wait_recv()
        parts = []
        for h in range(local // head):
            at = slice(h * head, (h + 1) * head)
            qh = qb[:, at]
            s = dot_nt(qh, kb[:, at]) * q_col * k_row
            s = jnp.where(allowed, s, -1e30)
            w = jnp.exp(s - jnp.max(s, axis=-1, keepdims=True))
            a = jnp.dot(
                w.astype(jnp.bfloat16), vb[:, at], preferred_element_type=jnp.float32
            ) / jnp.sum(w, axis=-1, keepdims=True)
            t = dot_nt(qh, tk[:, at]) * q_col
            w = jnp.exp(t - jnp.max(t, axis=-1, keepdims=True))
            b = jnp.dot(
                w.astype(jnp.bfloat16), tv[:, at], preferred_element_type=jnp.float32
            ) / jnp.sum(w, axis=-1, keepdims=True)
            parts.append(a + b)
        combined = jnp.where(mine, jnp.concatenate(parts, axis=1), 0.0).astype(jnp.bfloat16)
        gathered[2 * step, me] = combined
        gather(gathered.at[2 * step], 2 * step + 1)
        assemble(gathered.at[2 * step], full, 0, rows)
        if step == 0:
            loads[3].wait()
        projected = place(jnp.dot(full[...], wo[...], preferred_element_type=jnp.float32))
        for s in range(n):
            placed[s * span : (s + 1) * span, :] = jnp.broadcast_to(
                mods[2, s : s + 1, pl.ds(start_col, local)], (span, local)
            )
        state = jnp.where(
            mine, current[:, pl.ds(start_col, local)] + placed[...] * projected, 0.0
        )
        if step < STEPS - 1:
            gathered[2 * step + 1, me] = state.astype(jnp.bfloat16)
            gather(gathered.at[2 * step + 1], 2 * step + 2)
        else:
            osend[...] = state.reshape(n, span, local).astype(jnp.bfloat16)
            for k in range(1, n):
                target = lax.rem(me + k, n)
                c = remote(
                    osend.at[target],
                    orecv.at[me],
                    osend_sems.at[k],
                    orecv_sems.at[me],
                    target,
                )
                c.start()
                pending.append(c)
            orecv[me] = osend[me]
    for k in range(1, n):
        src = lax.rem(me + k, n)
        remote(
            osend.at[src], orecv.at[src], osend_sems.at[k], orecv_sems.at[src], sibling
        ).wait_recv()
    assemble(orecv, out, 0, span)
    for c in text:
        c.wait_send()
    drain()


def per_device_fused(
    hidden,
    incoming,
    levels,
    mod_table,
    query_weight,
    key_weight,
    value_weight,
    output_weight,
    query_gain,
    key_gain,
    text_keys,
    text_values,
):
    n = lax.axis_size("queue")
    span, width = hidden.shape
    cols = query_weight.shape[1]
    head = width // HEADS
    local = -(-cols // head) * head
    shared = 2 * local - 2 * cols
    rows = n * span
    text = n * text_keys.shape[0]
    mods = jnp.take(mod_table, levels, axis=0).transpose(1, 0, 2).astype(jnp.float32)
    vmem = pl.BlockSpec(memory_space=pltpu.VMEM)
    anywhere = pl.BlockSpec(memory_space=pl.ANY)
    dma = pltpu.SemaphoreType.DMA
    bf16, f32 = jnp.bfloat16, jnp.float32
    weight = pltpu.VMEM((width, cols), bf16)
    return pl.pallas_call(
        functools.partial(fused_kernel, n, cols),
        out_shape=jax.ShapeDtypeStruct((span, width), hidden.dtype),
        in_specs=[anywhere, vmem, vmem] + [anywhere] * 4 + [vmem] * 2 + [anywhere] * 2,
        out_specs=vmem,
        scratch_shapes=[
            weight,
            weight,
            weight,
            weight,
            pltpu.VMEM((n, span, width), bf16),
            pltpu.VMEM((2 * STEPS - 1, n, rows, local), bf16),
            pltpu.VMEM((rows, width), f32),
            pltpu.VMEM((rows, width), bf16),
            pltpu.VMEM((rows, local), f32),
            pltpu.VMEM((rows, local), bf16),
            pltpu.VMEM((rows, local), bf16),
            pltpu.VMEM((rows, local), bf16),
            pltpu.VMEM((STEPS, 2, rows, shared), bf16),
            pltpu.VMEM((STEPS, 2, rows, shared), bf16),
            pltpu.VMEM((STEPS, 2, 8, rows), f32),
            pltpu.VMEM((STEPS, n, 2, 8, rows), f32),
            pltpu.VMEM((text, local), bf16),
            pltpu.VMEM((text, local), bf16),
            pltpu.VMEM((n, span, local), bf16),
            pltpu.VMEM((n, span, local), bf16),
            dma((7,)),
            dma((2 * STEPS, n)),
            dma((2 * STEPS, n)),
            dma((STEPS, n)),
            dma((STEPS, n)),
            dma((STEPS,)),
            dma((STEPS,)),
            dma((2, n)),
            dma((2, n)),
            dma((n,)),
            dma((n,)),
        ],
        compiler_params=pltpu.CompilerParams(
            collective_id=0, has_side_effects=True, vmem_limit_bytes=60 * 1024 * 1024
        ),
    )(
        hidden,
        incoming,
        mods,
        query_weight,
        key_weight,
        value_weight,
        output_weight,
        query_gain.reshape(1, width),
        key_gain.reshape(1, width),
        text_keys,
        text_values,
    )


def fits_fused(count, rows_total, width, groups):
    head = width // HEADS
    cols = width // count
    span = rows_total // (count * groups)
    return (
        count % 4 == 0
        and head == 128
        and span == 8
        and (2 * cols) % head == 0
        and cols % head == head // 2
        and cols > head
        and count * span == 128
    )


def choose(mesh):
    def run(hidden, incoming, levels, mod_table, *rest):
        count = lax.axis_size("queue")
        if fits_fused(count, hidden.shape[0] * count, hidden.shape[1], 1):
            return per_device_fused(hidden, incoming, levels, mod_table, *rest)
        return per_device(hidden, incoming, levels, mod_table, *rest)

    return run


def solution(mesh):
    in_specs = (
        P(("groups", "queue"), None),
        P(None, "groups", None),
        P(),
        P(),
        P(None, "queue"),
        P(None, "queue"),
        P(None, "queue"),
        P(None, "queue"),
        P(),
        P(),
        P(("groups", "queue"), None),
        P(("groups", "queue"), None),
    )
    out_specs = P(("groups", "queue"), None)
    return jax.shard_map(
        choose(mesh), mesh=mesh, in_specs=in_specs, out_specs=out_specs, check_vma=False
    )
```

```python
import functools
import math

import jax
import jax.numpy as jnp
from jax import lax
from jax.experimental import pallas as pl
from jax.experimental.pallas import tpu as pltpu
from jax.sharding import PartitionSpec as P

HEADS = 40
STEPS = 2
FIRST_CHUNKS = 2
CHUNKS = 2


def passed_along(value, axis, steps):
    count = lax.axis_size(axis)
    initial, last = (max(0, -steps), min(count, count - steps))
    return lax.ppermute(value, axis, [(source, source + steps) for source in range(initial, last)])


def normalize(values):
    return values * lax.rsqrt(jnp.mean(values * values, axis=-1, keepdims=True) + 1e-06)


def softmax_rounded(scores):
    row_max = jnp.max(scores, axis=-1, keepdims=True)
    weights = jnp.exp(scores - row_max)
    return (weights / jnp.sum(weights, axis=-1, keepdims=True)).astype(jnp.bfloat16)


def pad_slots(values, slot_total):
    missing = slot_total - values.shape[1]
    filler = jnp.zeros((values.shape[0], missing, values.shape[2]), values.dtype)
    return jnp.concatenate([values, filler], axis=1)


def causal_block(queries, keys_all, values_all, span_rows, score_scale):
    total_rows = queries.shape[0]
    block_rows = min(512, total_rows)
    scores = (
        jnp.einsum("qsd,ksd->sqk", queries, keys_all, preferred_element_type=jnp.float32)
        * score_scale
    )
    allowed = (
        jnp.arange(0, block_rows)[:, None] // span_rows
        >= jnp.arange(block_rows)[None, :] // span_rows
    )
    scores = jnp.where(allowed[None], scores, -1e30)
    result = jnp.einsum(
        "sqk,ksd->qsd", softmax_rounded(scores), values_all, preferred_element_type=jnp.float32
    )
    pieces = result.astype(jnp.bfloat16)
    return pieces


def text_attend(queries, text_k, text_v, score_scale):
    scores = (
        jnp.einsum("qsd,tsd->sqt", queries, text_k, preferred_element_type=jnp.float32)
        * score_scale
    )
    return jnp.einsum(
        "sqt,tsd->qsd", softmax_rounded(scores), text_v, preferred_element_type=jnp.float32
    ).astype(jnp.bfloat16)


def per_device(
    hidden,
    incoming,
    levels,
    mod_table,
    query_weight,
    key_weight,
    value_weight,
    output_weight,
    query_gain,
    key_gain,
    text_keys,
    text_values,
):
    own_index = lax.axis_index("queue")
    queue_size = lax.axis_size("queue")
    span_rows, model_width = hidden.shape
    head_size = model_width // HEADS
    score_scale = 1.0 / math.sqrt(head_size)
    slot_total = -(-HEADS // queue_size) * queue_size
    own_level = lax.dynamic_index_in_dim(levels, own_index, 0, keepdims=False)
    modulation = lax.dynamic_index_in_dim(mod_table, own_level, 0, keepdims=False).astype(
        jnp.float32
    )
    stacked_weights = jnp.stack([query_weight, key_weight, value_weight])
    text_local = text_keys.shape[0]
    text_k_slots, text_v_slots = (
        lax.all_to_all(
            pad_slots(text_keys.reshape(text_local, HEADS, head_size), slot_total),
            "queue",
            split_axis=1,
            concat_axis=0,
            tiled=True,
        ),
        lax.all_to_all(
            pad_slots(text_values.reshape(text_local, HEADS, head_size), slot_total),
            "queue",
            split_axis=1,
            concat_axis=0,
            tiled=True,
        ),
    )
    queue_state = hidden
    for section_index in range(STEPS):
        shifted = passed_along(queue_state, "queue", 1)
        queue_state = jnp.where(own_index == 0, incoming[section_index], shifted)
        current = queue_state.astype(jnp.float32)
        modulated = (normalize(current) * (1.0 + modulation[1]) + modulation[0]).astype(
            jnp.bfloat16
        )
        columns = jnp.einsum(
            "rd,cdw->crw",
            lax.all_gather(modulated, "queue", axis=0, tiled=True),
            stacked_weights,
            preferred_element_type=jnp.float32,
        )
        own_rows = lax.all_to_all(
            columns.astype(jnp.bfloat16), "queue", split_axis=1, concat_axis=2, tiled=True
        ).astype(columns.dtype)
        query_heads = (
            (normalize(own_rows[0]) * query_gain)
            .astype(jnp.bfloat16)
            .reshape(span_rows, HEADS, head_size)
        )
        key_heads = (
            (normalize(own_rows[1]) * key_gain)
            .astype(jnp.bfloat16)
            .reshape(span_rows, HEADS, head_size)
        )
        value_heads = own_rows[2].astype(jnp.bfloat16).reshape(span_rows, HEADS, head_size)
        query_slots, key_slots, value_slots = (
            lax.all_to_all(
                pad_slots(query_heads, slot_total), "queue", split_axis=1, concat_axis=0, tiled=True
            ),
            lax.all_to_all(
                pad_slots(key_heads, slot_total), "queue", split_axis=1, concat_axis=0, tiled=True
            ),
            lax.all_to_all(
                pad_slots(value_heads, slot_total), "queue", split_axis=1, concat_axis=0, tiled=True
            ),
        )
        attended_slots = causal_block(query_slots, key_slots, value_slots, span_rows, score_scale)
        crossed_slots = text_attend(query_slots, text_k_slots, text_v_slots, score_scale)
        attended_back, crossed_back = (
            lax.all_to_all(attended_slots, "queue", split_axis=0, concat_axis=1, tiled=True),
            lax.all_to_all(crossed_slots, "queue", split_axis=0, concat_axis=1, tiled=True),
        )
        attended = attended_back[:, :HEADS]
        crossed = crossed_back[:, :HEADS]
        combined = (
            (attended.astype(jnp.float32) + crossed.astype(jnp.float32))
            .astype(jnp.bfloat16)
            .reshape(span_rows, model_width)
        )
        out_columns = jnp.dot(
            lax.all_gather(combined, "queue", axis=0, tiled=True),
            output_weight,
            preferred_element_type=jnp.float32,
        )
        projected = lax.all_to_all(
            out_columns.astype(jnp.bfloat16), "queue", split_axis=0, concat_axis=1, tiled=True
        ).astype(out_columns.dtype)
        queue_state = (current + modulation[2] * projected).astype(jnp.bfloat16)
    return queue_state


def dot_nt(a, b):
    return lax.dot_general(a, b, (((1,), (1,)), ((), ())), preferred_element_type=jnp.float32)


def fused_kernel(
    n,
    cols,
    hidden,
    incoming,
    levels,
    table_hbm,
    wq_hbm,
    wk_hbm,
    wv_hbm,
    wo_hbm,
    q_gain,
    k_gain,
    tkeys,
    tvals,
    out,
    table,
    mods,
    wq,
    wk,
    wv,
    wo,
    first,
    gathered,
    current,
    full,
    placed,
    qb,
    kb,
    vb,
    xsend,
    xrecv,
    ssend,
    srecv,
    tk,
    tv,
    osend,
    orecv,
    load_sems,
    gsend_sems,
    grecv_sems,
    ssend_sems,
    srecv_sems,
    xsend_sems,
    xrecv_sems,
    tsend_sems,
    trecv_sems,
    osend_sems,
    orecv_sems,
):
    me = lax.axis_index("queue")
    span, width = hidden.shape
    head = width // HEADS
    rows = n * span
    pair = 2 * cols
    local = placed.shape[1]
    blocks = gathered.shape[2]
    shared = 2 * local - pair
    step_off = pair - local
    core = lax.rem(me, 2)
    sibling = me + 1 - 2 * core
    across = me + 2 - 4 * lax.rem(me // 2, 2)
    outer = n // 4
    start_col = pl.multiple_of((me // 2) * pair + core * step_off, 128)
    mid = pl.multiple_of((1 - core) * step_off, 128)
    trows = tkeys.shape[0]
    scale = 1.0 / math.sqrt(head)

    loads = [
        pltpu.make_async_copy(s, d, load_sems.at[i])
        for i, (s, d) in enumerate(((wq_hbm, wq), (wk_hbm, wk), (wv_hbm, wv), (wo_hbm, wo)))
    ]
    own = pltpu.make_async_copy(hidden, first.at[me], load_sems.at[4])
    own.start()
    own_table = pltpu.make_async_copy(table_hbm, table, load_sems.at[7])
    own_table.start()
    own_tk = pltpu.make_async_copy(
        tkeys.at[:, pl.ds(start_col, local)], tk.at[pl.ds(me * trows, trows)], load_sems.at[5]
    )
    own_tv = pltpu.make_async_copy(
        tvals.at[:, pl.ds(start_col, local)], tv.at[pl.ds(me * trows, trows)], load_sems.at[6]
    )
    for item in loads + [own_tk, own_tv]:
        item.start()

    own.wait()
    barrier = pltpu.get_barrier_semaphore()
    for k in range(1, n):
        pl.semaphore_signal(
            barrier,
            inc=1,
            device_id={"queue": lax.rem(me + k, n)},
            device_id_type=pl.DeviceIdType.MESH,
        )
    pl.semaphore_wait(barrier, n - 1)

    pending = []

    def remote(src, dst, send, recv, target):
        return pltpu.make_async_remote_copy(
            src_ref=src,
            dst_ref=dst,
            send_sem=send,
            recv_sem=recv,
            device_id={"queue": target},
            device_id_type=pl.DeviceIdType.MESH,
        )

    def gather(view, chunks, phase, between=None):
        bank = phase % 2
        plane = lax.rem(me, 4)
        depth = me // 4

        def copy(slot, ch, kind, target):
            return remote(
                view(slot, ch),
                view(slot, ch),
                gsend_sems.at[bank, kind, slot, ch],
                grecv_sems.at[phase, slot, ch],
                target,
            )

        def push(slot, ch, kind, target):
            copy(slot, ch, kind, target).start()

        def arrived(slot, ch):
            copy(slot, ch, 3, sibling).wait_recv()

        def upward(slot, ch, act):
            @pl.when(depth < outer - 1)
            def _():
                act(copy(slot, ch, 0, lax.rem(me + 4, n)))

        def downward(slot, ch, act):
            @pl.when(depth > 0)
            def _():
                act(copy(slot, ch, 1, lax.rem(me + n - 4, n)))

        def start(c):
            c.start()

        for ch in range(chunks):
            upward(me, ch, start)
            downward(me, ch, start)
            push(me, ch, 2, across)
            push(me, ch, 3, sibling)

        def line(act_in, act_up, act_down, act_side):
            for d in range(1, outer):
                for ch in range(chunks):

                    @pl.when(depth >= d)
                    def _():
                        slot = lax.rem(me + n - 4 * d, n)
                        act_in(slot, ch)
                        upward(slot, ch, act_up)
                        act_side(slot, ch)

                    @pl.when(depth < outer - d)
                    def _():
                        slot = lax.rem(me + 4 * d, n)
                        act_in(slot, ch)
                        downward(slot, ch, act_down)
                        act_side(slot, ch)

        def sides(slot, ch):
            push(slot, ch, 2, across)
            push(slot, ch, 3, sibling)

        line(arrived, start, start, sides)
        if between is not None:
            between()

        far = [0] + list(range(1, outer))
        for d in far:
            for ch in range(chunks):
                slot = lax.rem(across + n - 4 * d, n)
                arrived(slot, ch)
                push(slot, ch, 3, sibling)
        opposite = me + 3 - 2 * plane
        for base in (sibling, opposite):
            for d in far:
                for ch in range(chunks):
                    arrived(lax.rem(base + n - 4 * d, n), ch)

        def sent(c):
            c.wait_send()

        def finish():
            for ch in range(chunks):
                upward(me, ch, sent)
                downward(me, ch, sent)
                copy(me, ch, 2, across).wait_send()
                copy(me, ch, 3, sibling).wait_send()

            def sides_sent(slot, ch):
                copy(slot, ch, 2, across).wait_send()
                copy(slot, ch, 3, sibling).wait_send()

            line(lambda slot, ch: None, sent, sent, sides_sent)
            for d in far:
                for ch in range(chunks):
                    copy(lax.rem(across + n - 4 * d, n), ch, 3, sibling).wait_send()

        return finish

    def drain():
        for c in pending:
            c.wait_send()
        pending.clear()

    def pack(value, dst):
        placed[...] = value
        dst[:rows, :] = placed[:, pl.ds(pl.multiple_of(core * shared, 128), step_off)].astype(
            jnp.bfloat16
        )
        half = rows // 2
        folded = placed[:half, pl.ds(mid, shared)] + pltpu.roll(
            placed[half:, pl.ds(mid, shared)], shared // 2, 1
        )
        fold = half * shared // step_off
        for e in range(step_off // shared):
            dst[rows:, e * shared : (e + 1) * shared] = folded[
                e * fold : (e + 1) * fold
            ].astype(jnp.bfloat16)

    low = lax.broadcasted_iota(jnp.int32, (rows // 2, shared), 1) < shared // 2

    def unpack(buf, dst, base, count):
        for p in range(n // 2):
            a, b = buf.at[2 * p], buf.at[2 * p + 1]
            at = p * pair
            half = rows // 2
            dst[pl.ds(base, count), at : at + step_off] = a[:count, :].astype(dst.dtype)
            dst[pl.ds(base, count), at + local : at + pair] = b[:count, :].astype(dst.dtype)
            fa, fb = (
                jnp.concatenate(
                    [
                        r[rows:, e * shared : (e + 1) * shared].astype(jnp.float32)
                        for e in range(step_off // shared)
                    ],
                    axis=0,
                )
                for r in (a, b)
            )
            at = at + step_off
            dst[pl.ds(base, half), at : at + shared] = jnp.where(low, fa, fb).astype(dst.dtype)
            rest = pltpu.roll(jnp.where(low, fb, fa), shared // 2, 1)
            dst[pl.ds(base + half, count - half), at : at + shared] = rest[
                : count - half
            ].astype(dst.dtype)

    lane = lax.broadcasted_iota(jnp.int32, (rows, local), 1)
    shift = core * (local - cols)
    mine = (lane >= shift) & (lane < shift + cols)

    def place(value):
        placed[:, :cols] = value
        placed[:, cols:] = jnp.zeros((rows, local - cols), jnp.float32)
        y = placed[...]
        return jnp.where(mine, jnp.where(core == 1, pltpu.roll(y, local - cols, 1), y), 0.0)

    def assemble(buf, dst, base, count):
        for p in range(n // 2):
            a = buf[2 * p, :count]
            b = buf[2 * p + 1, :count]
            at = p * pair
            kept = pl.ds(base, count)
            dst[kept, at : at + step_off] = a[:, :step_off].astype(dst.dtype)
            dst[kept, at + step_off : at + local] = (
                a[:, step_off:].astype(jnp.float32) + b[:, :shared].astype(jnp.float32)
            ).astype(dst.dtype)
            dst[kept, at + local : at + pair] = b[:, shared:].astype(dst.dtype)

    def modulate():
        def body(i, carry):
            r0 = pl.multiple_of(i * 2 * span, 2 * span)
            c = current[pl.ds(r0, 2 * span), :]
            c = c * lax.rsqrt(jnp.mean(c * c, axis=-1, keepdims=True) + 1e-06)

            def rows_of(kind):
                return jnp.concatenate(
                    [
                        jnp.broadcast_to(mods[kind, pl.ds(2 * i + e, 1), :], (span, width))
                        for e in range(2)
                    ],
                    axis=0,
                )

            full[pl.ds(r0, 2 * span), :] = (c * (1.0 + rows_of(1)) + rows_of(0)).astype(
                jnp.bfloat16
            )
            return carry

        lax.fori_loop(0, n // 2, body, 0)

    qg = q_gain[:, pl.ds(start_col, local)]
    kg = k_gain[:, pl.ds(start_col, local)]
    ones = jnp.ones((8, local), jnp.float32)
    allowed = (
        lax.broadcasted_iota(jnp.int32, (rows, rows), 0) // span
        >= lax.broadcasted_iota(jnp.int32, (rows, rows), 1) // span
    )

    text = []

    def send_text():
        for k in range(1, n):
            target = lax.rem(me + k, n)
            col = pl.multiple_of((target // 2) * pair + lax.rem(target, 2) * step_off, 128)
            for kind, (s, d) in enumerate(((tkeys, tk), (tvals, tv))):
                c = remote(
                    s.at[:, pl.ds(col, local)],
                    d.at[pl.ds(me * trows, trows)],
                    tsend_sems.at[kind, k],
                    trecv_sems.at[kind, me],
                    target,
                )
                c.start()
                text.append(c)

    def prepare():
        send_text()
        own_table.wait()
        picks = (
            lax.broadcasted_iota(jnp.int32, (table.shape[1], n), 0) == levels[...]
        ).astype(jnp.float32)
        picks = jnp.transpose(picks).astype(jnp.bfloat16)
        for kind in range(3):
            mods[kind] = jnp.dot(picks, table[kind], preferred_element_type=jnp.float32)

    part = width // FIRST_CHUNKS
    finish = gather(
        lambda slot, ch: first.at[slot, :, pl.ds(ch * part, part)], FIRST_CHUNKS, 0, prepare
    )
    piece = blocks // CHUNKS

    def block_view(phase):
        return lambda slot, ch: gathered.at[phase, slot, pl.ds(ch * piece, piece)]

    for step in range(STEPS):
        current[0:span, :] = incoming[step].astype(jnp.float32)
        if step == 0:
            for s in range(1, n):
                current[s * span : (s + 1) * span, :] = first[s - 1].astype(jnp.float32)
        else:
            unpack(gathered.at[2 * step - 1], current, span, rows - span)
        modulate()
        if step == 0:
            loads[0].wait()
            loads[1].wait()
        m = full[...]
        q = place(dot_nt(m, wq[...]))
        ssend[step, 0] = dot_nt(ones, q * q)
        qb[...] = (q * qg).astype(jnp.bfloat16)
        k_ = place(dot_nt(m, wk[...]))
        ssend[step, 1] = dot_nt(ones, k_ * k_)
        kb[...] = (k_ * kg).astype(jnp.bfloat16)
        for k in range(1, n):
            c = remote(
                ssend.at[step],
                srecv.at[step, me],
                ssend_sems.at[step, k],
                srecv_sems.at[step, me],
                lax.rem(me + k, n),
            )
            c.start()
            pending.append(c)
        srecv[step, me] = ssend[step]
        xsend[step, 0] = qb[:, pl.ds(mid, shared)]
        xsend[step, 1] = kb[:, pl.ds(mid, shared)]
        swap = remote(
            xsend.at[step], xrecv.at[step], xsend_sems.at[step], xrecv_sems.at[step], sibling
        )
        swap.start()
        if step == 0:
            loads[2].wait()
        vb[...] = place(dot_nt(m, wv[...])).astype(
            jnp.bfloat16
        )
        swap.wait()
        qb[:, pl.ds(mid, shared)] = qb[:, pl.ds(mid, shared)] + xrecv[step, 0]
        kb[:, pl.ds(mid, shared)] = kb[:, pl.ds(mid, shared)] + xrecv[step, 1]
        for k in range(1, n):
            src = lax.rem(me + k, n)
            remote(
                ssend.at[step],
                srecv.at[step, src],
                ssend_sems.at[step, k],
                srecv_sems.at[step, src],
                sibling,
            ).wait_recv()
        total = jnp.sum(srecv[step], axis=0)
        inv = lax.rsqrt(total * (1.0 / width) + 1e-06)
        q_col = jnp.transpose(jnp.broadcast_to(inv[0, 0:1], (128, rows)))[:, 0:1] * scale
        k_row = inv[1, 0:1]
        if step == 0:
            own_tk.wait()
            own_tv.wait()
            for k in range(1, n):
                src = lax.rem(me + k, n)
                for kind, d in enumerate((tk, tv)):
                    remote(
                        d.at[pl.ds(src * trows, trows)],
                        d.at[pl.ds(src * trows, trows)],
                        tsend_sems.at[kind, k],
                        trecv_sems.at[kind, src],
                        sibling,
                    ).wait_recv()
        parts = []
        for h in range(local // head):
            at = slice(h * head, (h + 1) * head)
            qh = qb[:, at]
            s = dot_nt(qh, kb[:, at]) * q_col * k_row
            s = jnp.where(allowed, s, -1e30)
            w = jnp.exp(s - jnp.max(s, axis=-1, keepdims=True))
            a = jnp.dot(
                w.astype(jnp.bfloat16), vb[:, at], preferred_element_type=jnp.float32
            ) / jnp.sum(w, axis=-1, keepdims=True)
            t = dot_nt(qh, tk[:, at]) * q_col
            w = jnp.exp(t - jnp.max(t, axis=-1, keepdims=True))
            b = jnp.dot(
                w.astype(jnp.bfloat16), tv[:, at], preferred_element_type=jnp.float32
            ) / jnp.sum(w, axis=-1, keepdims=True)
            parts.append(a + b)
        pack(
            jnp.where(mine, jnp.concatenate(parts, axis=1), 0.0), gathered.at[2 * step, me]
        )
        finish()
        finish = gather(block_view(2 * step), CHUNKS, 2 * step + 1)
        unpack(gathered.at[2 * step], full, 0, rows)
        if step == 0:
            loads[3].wait()
        projected = place(dot_nt(full[...], wo[...]))
        for s in range(n):
            placed[s * span : (s + 1) * span, :] = jnp.broadcast_to(
                mods[2, s : s + 1, pl.ds(start_col, local)], (span, local)
            )
        state = jnp.where(
            mine, current[:, pl.ds(start_col, local)] + placed[...] * projected, 0.0
        )
        if step < STEPS - 1:
            pack(state, gathered.at[2 * step + 1, me])
            finish()
            finish = gather(block_view(2 * step + 1), CHUNKS, 2 * step + 2)
        else:
            osend[...] = state.reshape(n, span, local).astype(jnp.bfloat16)
            for k in range(1, n):
                target = lax.rem(me + k, n)
                c = remote(
                    osend.at[target],
                    orecv.at[me],
                    osend_sems.at[k],
                    orecv_sems.at[me],
                    target,
                )
                c.start()
                pending.append(c)
            orecv[me] = osend[me]
    for k in range(1, n):
        src = lax.rem(me + k, n)
        remote(
            osend.at[src], orecv.at[src], osend_sems.at[k], orecv_sems.at[src], sibling
        ).wait_recv()
    assemble(orecv, out, 0, span)
    for c in text:
        c.wait_send()
    finish()
    drain()


def per_device_fused(
    hidden,
    incoming,
    levels,
    mod_table,
    query_weight,
    key_weight,
    value_weight,
    output_weight,
    query_gain,
    key_gain,
    text_keys,
    text_values,
):
    n = lax.axis_size("queue")
    span, width = hidden.shape
    cols = query_weight.shape[1]
    head = width // HEADS
    local = -(-cols // head) * head
    shared = 2 * local - 2 * cols
    step_off = 2 * cols - local
    rows = n * span
    text = n * text_keys.shape[0]
    vmem = pl.BlockSpec(memory_space=pltpu.VMEM)
    anywhere = pl.BlockSpec(memory_space=pl.ANY)
    dma = pltpu.SemaphoreType.DMA
    bf16, f32 = jnp.bfloat16, jnp.float32
    weight = pltpu.VMEM((cols, width), bf16)
    most = max(FIRST_CHUNKS, CHUNKS)
    return pl.pallas_call(
        functools.partial(fused_kernel, n, cols),
        out_shape=jax.ShapeDtypeStruct((span, width), hidden.dtype),
        in_specs=[anywhere, vmem, vmem] + [anywhere] * 5 + [vmem] * 2 + [anywhere] * 2,
        out_specs=vmem,
        scratch_shapes=[
            pltpu.VMEM((3, mod_table.shape[0], width), bf16),
            pltpu.VMEM((3, n, width), f32),
            weight,
            weight,
            weight,
            weight,
            pltpu.VMEM((n, span, width), bf16),
            pltpu.VMEM((2 * STEPS - 1, n, rows * cols // step_off, step_off), bf16),
            pltpu.VMEM((rows, width), f32),
            pltpu.VMEM((rows, width), bf16),
            pltpu.VMEM((rows, local), f32),
            pltpu.VMEM((rows, local), bf16),
            pltpu.VMEM((rows, local), bf16),
            pltpu.VMEM((rows, local), bf16),
            pltpu.VMEM((STEPS, 2, rows, shared), bf16),
            pltpu.VMEM((STEPS, 2, rows, shared), bf16),
            pltpu.VMEM((STEPS, 2, 8, rows), f32),
            pltpu.VMEM((STEPS, n, 2, 8, rows), f32),
            pltpu.VMEM((text, local), bf16),
            pltpu.VMEM((text, local), bf16),
            pltpu.VMEM((n, span, local), bf16),
            pltpu.VMEM((n, span, local), bf16),
            dma((8,)),
            dma((2, 4, n, most)),
            dma((2 * STEPS, n, most)),
            dma((STEPS, n)),
            dma((STEPS, n)),
            dma((STEPS,)),
            dma((STEPS,)),
            dma((2, n)),
            dma((2, n)),
            dma((n,)),
            dma((n,)),
        ],
        compiler_params=pltpu.CompilerParams(
            collective_id=0, has_side_effects=True, vmem_limit_bytes=60 * 1024 * 1024
        ),
    )(
        hidden,
        incoming,
        levels.reshape(1, n),
        mod_table.transpose(1, 0, 2),
        query_weight.T,
        key_weight.T,
        value_weight.T,
        output_weight.T,
        query_gain.reshape(1, width),
        key_gain.reshape(1, width),
        text_keys,
        text_values,
    )


def fits_fused(count, rows_total, width, groups):
    head = width // HEADS
    cols = width // count
    span = rows_total // (count * groups)
    return (
        count % 4 == 0
        and head == 128
        and span == 8
        and (2 * cols) % head == 0
        and cols % head == head // 2
        and cols > head
        and count * span == 128
    )


def choose(mesh):
    def run(hidden, incoming, levels, mod_table, *rest):
        count = lax.axis_size("queue")
        if fits_fused(count, hidden.shape[0] * count, hidden.shape[1], 1):
            return per_device_fused(hidden, incoming, levels, mod_table, *rest)
        return per_device(hidden, incoming, levels, mod_table, *rest)

    return run


def solution(mesh):
    in_specs = (
        P(("groups", "queue"), None),
        P(None, "groups", None),
        P(),
        P(),
        P(None, "queue"),
        P(None, "queue"),
        P(None, "queue"),
        P(None, "queue"),
        P(),
        P(),
        P(("groups", "queue"), None),
        P(("groups", "queue"), None),
    )
    out_specs = P(("groups", "queue"), None)
    return jax.shard_map(
        choose(mesh), mesh=mesh, in_specs=in_specs, out_specs=out_specs, check_vma=False
    )
```

```python
import functools
import math

import jax
import jax.numpy as jnp
from jax import lax
from jax.experimental import pallas as pl
from jax.experimental.pallas import tpu as pltpu
from jax.sharding import PartitionSpec as P

HEADS = 40
STEPS = 2
FIRST_CHUNKS = 2
CHUNKS = 2


def passed_along(value, axis, steps):
    count = lax.axis_size(axis)
    initial, last = (max(0, -steps), min(count, count - steps))
    return lax.ppermute(value, axis, [(source, source + steps) for source in range(initial, last)])


def normalize(values):
    return values * lax.rsqrt(jnp.mean(values * values, axis=-1, keepdims=True) + 1e-06)


def softmax_rounded(scores):
    row_max = jnp.max(scores, axis=-1, keepdims=True)
    weights = jnp.exp(scores - row_max)
    return (weights / jnp.sum(weights, axis=-1, keepdims=True)).astype(jnp.bfloat16)


def pad_slots(values, slot_total):
    missing = slot_total - values.shape[1]
    filler = jnp.zeros((values.shape[0], missing, values.shape[2]), values.dtype)
    return jnp.concatenate([values, filler], axis=1)


def causal_block(queries, keys_all, values_all, span_rows, score_scale):
    total_rows = queries.shape[0]
    block_rows = min(512, total_rows)
    scores = (
        jnp.einsum("qsd,ksd->sqk", queries, keys_all, preferred_element_type=jnp.float32)
        * score_scale
    )
    allowed = (
        jnp.arange(0, block_rows)[:, None] // span_rows
        >= jnp.arange(block_rows)[None, :] // span_rows
    )
    scores = jnp.where(allowed[None], scores, -1e30)
    result = jnp.einsum(
        "sqk,ksd->qsd", softmax_rounded(scores), values_all, preferred_element_type=jnp.float32
    )
    pieces = result.astype(jnp.bfloat16)
    return pieces


def text_attend(queries, text_k, text_v, score_scale):
    scores = (
        jnp.einsum("qsd,tsd->sqt", queries, text_k, preferred_element_type=jnp.float32)
        * score_scale
    )
    return jnp.einsum(
        "sqt,tsd->qsd", softmax_rounded(scores), text_v, preferred_element_type=jnp.float32
    ).astype(jnp.bfloat16)


def per_device(
    hidden,
    incoming,
    levels,
    mod_table,
    query_weight,
    key_weight,
    value_weight,
    output_weight,
    query_gain,
    key_gain,
    text_keys,
    text_values,
):
    own_index = lax.axis_index("queue")
    queue_size = lax.axis_size("queue")
    span_rows, model_width = hidden.shape
    head_size = model_width // HEADS
    score_scale = 1.0 / math.sqrt(head_size)
    slot_total = -(-HEADS // queue_size) * queue_size
    own_level = lax.dynamic_index_in_dim(levels, own_index, 0, keepdims=False)
    modulation = lax.dynamic_index_in_dim(mod_table, own_level, 0, keepdims=False).astype(
        jnp.float32
    )
    stacked_weights = jnp.stack([query_weight, key_weight, value_weight])
    text_local = text_keys.shape[0]
    text_k_slots, text_v_slots = (
        lax.all_to_all(
            pad_slots(text_keys.reshape(text_local, HEADS, head_size), slot_total),
            "queue",
            split_axis=1,
            concat_axis=0,
            tiled=True,
        ),
        lax.all_to_all(
            pad_slots(text_values.reshape(text_local, HEADS, head_size), slot_total),
            "queue",
            split_axis=1,
            concat_axis=0,
            tiled=True,
        ),
    )
    queue_state = hidden
    for section_index in range(STEPS):
        shifted = passed_along(queue_state, "queue", 1)
        queue_state = jnp.where(own_index == 0, incoming[section_index], shifted)
        current = queue_state.astype(jnp.float32)
        modulated = (normalize(current) * (1.0 + modulation[1]) + modulation[0]).astype(
            jnp.bfloat16
        )
        columns = jnp.einsum(
            "rd,cdw->crw",
            lax.all_gather(modulated, "queue", axis=0, tiled=True),
            stacked_weights,
            preferred_element_type=jnp.float32,
        )
        own_rows = lax.all_to_all(
            columns.astype(jnp.bfloat16), "queue", split_axis=1, concat_axis=2, tiled=True
        ).astype(columns.dtype)
        query_heads = (
            (normalize(own_rows[0]) * query_gain)
            .astype(jnp.bfloat16)
            .reshape(span_rows, HEADS, head_size)
        )
        key_heads = (
            (normalize(own_rows[1]) * key_gain)
            .astype(jnp.bfloat16)
            .reshape(span_rows, HEADS, head_size)
        )
        value_heads = own_rows[2].astype(jnp.bfloat16).reshape(span_rows, HEADS, head_size)
        query_slots, key_slots, value_slots = (
            lax.all_to_all(
                pad_slots(query_heads, slot_total), "queue", split_axis=1, concat_axis=0, tiled=True
            ),
            lax.all_to_all(
                pad_slots(key_heads, slot_total), "queue", split_axis=1, concat_axis=0, tiled=True
            ),
            lax.all_to_all(
                pad_slots(value_heads, slot_total), "queue", split_axis=1, concat_axis=0, tiled=True
            ),
        )
        attended_slots = causal_block(query_slots, key_slots, value_slots, span_rows, score_scale)
        crossed_slots = text_attend(query_slots, text_k_slots, text_v_slots, score_scale)
        attended_back, crossed_back = (
            lax.all_to_all(attended_slots, "queue", split_axis=0, concat_axis=1, tiled=True),
            lax.all_to_all(crossed_slots, "queue", split_axis=0, concat_axis=1, tiled=True),
        )
        attended = attended_back[:, :HEADS]
        crossed = crossed_back[:, :HEADS]
        combined = (
            (attended.astype(jnp.float32) + crossed.astype(jnp.float32))
            .astype(jnp.bfloat16)
            .reshape(span_rows, model_width)
        )
        out_columns = jnp.dot(
            lax.all_gather(combined, "queue", axis=0, tiled=True),
            output_weight,
            preferred_element_type=jnp.float32,
        )
        projected = lax.all_to_all(
            out_columns.astype(jnp.bfloat16), "queue", split_axis=0, concat_axis=1, tiled=True
        ).astype(out_columns.dtype)
        queue_state = (current + modulation[2] * projected).astype(jnp.bfloat16)
    return queue_state


def dot_nt(a, b):
    return lax.dot_general(a, b, (((1,), (1,)), ((), ())), preferred_element_type=jnp.float32)


def fused_kernel(
    n,
    cols,
    hidden,
    incoming,
    levels,
    table_hbm,
    wq_hbm,
    wk_hbm,
    wv_hbm,
    wo_hbm,
    q_gain,
    k_gain,
    tkeys,
    tvals,
    out,
    table,
    mods,
    wq,
    wk,
    wv,
    wo,
    first,
    gathered,
    current,
    full,
    placed,
    qb,
    kb,
    vb,
    xsend,
    xrecv,
    ssend,
    srecv,
    tk,
    tv,
    osend,
    orecv,
    load_sems,
    gsend_sems,
    grecv_sems,
    ssend_sems,
    srecv_sems,
    xsend_sems,
    xrecv_sems,
    tsend_sems,
    trecv_sems,
    osend_sems,
    orecv_sems,
):
    me = lax.axis_index("queue")
    span, width = hidden.shape
    head = width // HEADS
    rows = n * span
    pair = 2 * cols
    local = placed.shape[1]
    blocks = gathered.shape[2]
    shared = 2 * local - pair
    step_off = pair - local
    core = lax.rem(me, 2)
    sibling = me + 1 - 2 * core
    across = me + 2 - 4 * lax.rem(me // 2, 2)
    outer = n // 4
    start_col = pl.multiple_of((me // 2) * pair + core * step_off, 128)
    mid = pl.multiple_of((1 - core) * step_off, 128)
    trows = tkeys.shape[0]
    scale = 1.0 / math.sqrt(head)

    loads = [
        pltpu.make_async_copy(s, d, load_sems.at[i])
        for i, (s, d) in enumerate(((wq_hbm, wq), (wk_hbm, wk), (wv_hbm, wv), (wo_hbm, wo)))
    ]
    own = pltpu.make_async_copy(hidden, first.at[me], load_sems.at[4])
    own.start()
    own_table = pltpu.make_async_copy(table_hbm, table, load_sems.at[7])
    own_table.start()
    own_tk = pltpu.make_async_copy(
        tkeys.at[:, pl.ds(start_col, local)], tk.at[pl.ds(me * trows, trows)], load_sems.at[5]
    )
    own_tv = pltpu.make_async_copy(
        tvals.at[:, pl.ds(start_col, local)], tv.at[pl.ds(me * trows, trows)], load_sems.at[6]
    )
    for item in loads + [own_tk, own_tv]:
        item.start()

    own.wait()
    barrier = pltpu.get_barrier_semaphore()
    for k in range(1, n):
        pl.semaphore_signal(
            barrier,
            inc=1,
            device_id={"queue": lax.rem(me + k, n)},
            device_id_type=pl.DeviceIdType.MESH,
        )
    pl.semaphore_wait(barrier, n - 1)

    pending = []

    def remote(src, dst, send, recv, target):
        return pltpu.make_async_remote_copy(
            src_ref=src,
            dst_ref=dst,
            send_sem=send,
            recv_sem=recv,
            device_id={"queue": target},
            device_id_type=pl.DeviceIdType.MESH,
        )

    def gather(view, chunks, phase, between=None):
        bank = phase % 2
        plane = lax.rem(me, 4)
        depth = me // 4

        def copy(slot, ch, kind, target):
            return remote(
                view(slot, ch),
                view(slot, ch),
                gsend_sems.at[bank, kind, slot, ch],
                grecv_sems.at[phase, slot, ch],
                target,
            )

        def push(slot, ch, kind, target):
            copy(slot, ch, kind, target).start()

        def arrived(slot, ch):
            copy(slot, ch, 3, sibling).wait_recv()

        def upward(slot, ch, act):
            @pl.when(depth < outer - 1)
            def _():
                act(copy(slot, ch, 0, lax.rem(me + 4, n)))

        def downward(slot, ch, act):
            @pl.when(depth > 0)
            def _():
                act(copy(slot, ch, 1, lax.rem(me + n - 4, n)))

        def start(c):
            c.start()

        for ch in range(chunks):
            upward(me, ch, start)
            downward(me, ch, start)
            push(me, ch, 2, across)
            push(me, ch, 3, sibling)

        def line(act_in, act_up, act_down, act_side, after=None):
            for d in range(1, outer):
                for ch in range(chunks):

                    @pl.when(depth >= d)
                    def _():
                        slot = lax.rem(me + n - 4 * d, n)
                        act_in(slot, ch)
                        upward(slot, ch, act_up)
                        act_side(slot, ch)

                    @pl.when(depth < outer - d)
                    def _():
                        slot = lax.rem(me + 4 * d, n)
                        act_in(slot, ch)
                        downward(slot, ch, act_down)
                        act_side(slot, ch)
                if after is not None:
                    after(d - 1)

        def sides(slot, ch):
            push(slot, ch, 2, across)
            push(slot, ch, 3, sibling)

        far = [0] + list(range(1, outer))

        def relay(slot, ch):
            arrived(slot, ch)
            push(slot, ch, 3, sibling)

        def other_row(d):
            if d == outer - 2 and between is not None:
                between()
            for ch in range(chunks):
                if d == 0:
                    relay(across, ch)
                else:

                    @pl.when(depth >= d)
                    def _():
                        relay(lax.rem(across + n - 4 * d, n), ch)

                    @pl.when(depth < outer - d)
                    def _():
                        relay(lax.rem(across + 4 * d, n), ch)

        line(arrived, start, start, sides, other_row)
        other_row(outer - 1)
        opposite = me + 3 - 2 * plane
        for base in (sibling, opposite):
            for d in far:
                for ch in range(chunks):
                    arrived(lax.rem(base + n - 4 * d, n), ch)

        def sent(c):
            c.wait_send()

        def finish():
            for ch in range(chunks):
                upward(me, ch, sent)
                downward(me, ch, sent)
                copy(me, ch, 2, across).wait_send()
                copy(me, ch, 3, sibling).wait_send()

            def sides_sent(slot, ch):
                copy(slot, ch, 2, across).wait_send()
                copy(slot, ch, 3, sibling).wait_send()

            line(lambda slot, ch: None, sent, sent, sides_sent)
            for d in far:
                for ch in range(chunks):
                    copy(lax.rem(across + n - 4 * d, n), ch, 3, sibling).wait_send()

        return finish

    def drain():
        for c in pending:
            c.wait_send()
        pending.clear()

    def pack(value, dst):
        placed[...] = value
        dst[:rows, :] = placed[:, pl.ds(pl.multiple_of(core * shared, 128), step_off)].astype(
            jnp.bfloat16
        )
        half = rows // 2
        folded = placed[:half, pl.ds(mid, shared)] + pltpu.roll(
            placed[half:, pl.ds(mid, shared)], shared // 2, 1
        )
        fold = half * shared // step_off
        for e in range(step_off // shared):
            dst[rows:, e * shared : (e + 1) * shared] = folded[
                e * fold : (e + 1) * fold
            ].astype(jnp.bfloat16)

    low = lax.broadcasted_iota(jnp.int32, (rows // 2, shared), 1) < shared // 2

    def unpack(buf, dst, base, count):
        for p in range(n // 2):
            a, b = buf.at[2 * p], buf.at[2 * p + 1]
            at = p * pair
            half = rows // 2
            dst[pl.ds(base, count), at : at + step_off] = a[:count, :].astype(dst.dtype)
            dst[pl.ds(base, count), at + local : at + pair] = b[:count, :].astype(dst.dtype)
            fa, fb = (
                jnp.concatenate(
                    [
                        r[rows:, e * shared : (e + 1) * shared].astype(jnp.float32)
                        for e in range(step_off // shared)
                    ],
                    axis=0,
                )
                for r in (a, b)
            )
            at = at + step_off
            dst[pl.ds(base, half), at : at + shared] = jnp.where(low, fa, fb).astype(dst.dtype)
            rest = pltpu.roll(jnp.where(low, fb, fa), shared // 2, 1)
            dst[pl.ds(base + half, count - half), at : at + shared] = rest[
                : count - half
            ].astype(dst.dtype)

    lane = lax.broadcasted_iota(jnp.int32, (rows, local), 1)
    shift = core * (local - cols)
    mine = (lane >= shift) & (lane < shift + cols)

    def place(value):
        placed[:, :cols] = value
        placed[:, cols:] = jnp.zeros((rows, local - cols), jnp.float32)
        y = placed[...]
        return jnp.where(mine, jnp.where(core == 1, pltpu.roll(y, local - cols, 1), y), 0.0)

    def assemble(buf, dst, base, count):
        for p in range(n // 2):
            a = buf[2 * p, :count]
            b = buf[2 * p + 1, :count]
            at = p * pair
            kept = pl.ds(base, count)
            dst[kept, at : at + step_off] = a[:, :step_off].astype(dst.dtype)
            dst[kept, at + step_off : at + local] = (
                a[:, step_off:].astype(jnp.float32) + b[:, :shared].astype(jnp.float32)
            ).astype(dst.dtype)
            dst[kept, at + local : at + pair] = b[:, shared:].astype(dst.dtype)

    def modulate():
        def body(i, carry):
            r0 = pl.multiple_of(i * 2 * span, 2 * span)
            c = current[pl.ds(r0, 2 * span), :]
            c = c * lax.rsqrt(jnp.mean(c * c, axis=-1, keepdims=True) + 1e-06)

            def rows_of(kind):
                return jnp.concatenate(
                    [
                        jnp.broadcast_to(mods[kind, pl.ds(2 * i + e, 1), :], (span, width))
                        for e in range(2)
                    ],
                    axis=0,
                )

            full[pl.ds(r0, 2 * span), :] = (c * (1.0 + rows_of(1)) + rows_of(0)).astype(
                jnp.bfloat16
            )
            return carry

        lax.fori_loop(0, n // 2, body, 0)

    qg = q_gain[:, pl.ds(start_col, local)]
    kg = k_gain[:, pl.ds(start_col, local)]
    ones = jnp.ones((8, local), jnp.float32)
    allowed = (
        lax.broadcasted_iota(jnp.int32, (rows, rows), 0) // span
        >= lax.broadcasted_iota(jnp.int32, (rows, rows), 1) // span
    )

    text = []

    def send_text():
        for k in range(1, n):
            target = lax.rem(me + k, n)
            col = pl.multiple_of((target // 2) * pair + lax.rem(target, 2) * step_off, 128)
            for kind, (s, d) in enumerate(((tkeys, tk), (tvals, tv))):
                c = remote(
                    s.at[:, pl.ds(col, local)],
                    d.at[pl.ds(me * trows, trows)],
                    tsend_sems.at[kind, k],
                    trecv_sems.at[kind, me],
                    target,
                )
                c.start()
                text.append(c)

    def prepare():
        send_text()
        own_table.wait()
        picks = (
            lax.broadcasted_iota(jnp.int32, (table.shape[1], n), 0) == levels[...]
        ).astype(jnp.float32)
        picks = jnp.transpose(picks).astype(jnp.bfloat16)
        for kind in range(3):
            mods[kind] = jnp.dot(picks, table[kind], preferred_element_type=jnp.float32)

    part = width // FIRST_CHUNKS
    finish = gather(
        lambda slot, ch: first.at[slot, :, pl.ds(ch * part, part)], FIRST_CHUNKS, 0, prepare
    )
    piece = blocks // CHUNKS

    def block_view(phase):
        return lambda slot, ch: gathered.at[phase, slot, pl.ds(ch * piece, piece)]

    for step in range(STEPS):
        current[0:span, :] = incoming[step].astype(jnp.float32)
        if step == 0:
            for s in range(1, n):
                current[s * span : (s + 1) * span, :] = first[s - 1].astype(jnp.float32)
        else:
            unpack(gathered.at[2 * step - 1], current, span, rows - span)
        modulate()
        if step == 0:
            loads[0].wait()
            loads[1].wait()
        m = full[...]
        q = place(dot_nt(m, wq[...]))
        ssend[step, 0:1] = dot_nt(ones, q * q)[0:1]
        qb[...] = (q * qg).astype(jnp.bfloat16)
        k_ = place(dot_nt(m, wk[...]))
        ssend[step, 1:2] = dot_nt(ones, k_ * k_)[0:1]
        kb[...] = (k_ * kg).astype(jnp.bfloat16)
        for k in range(1, n):
            c = remote(
                ssend.at[step],
                srecv.at[step, me],
                ssend_sems.at[step, k],
                srecv_sems.at[step, me],
                lax.rem(me + k, n),
            )
            c.start()
            pending.append(c)
        srecv[step, me] = ssend[step]
        xsend[step, 0] = qb[:, pl.ds(mid, shared)]
        xsend[step, 1] = kb[:, pl.ds(mid, shared)]
        swap = remote(
            xsend.at[step], xrecv.at[step], xsend_sems.at[step], xrecv_sems.at[step], sibling
        )
        swap.start()
        if step == 0:
            loads[2].wait()
        vb[...] = place(dot_nt(m, wv[...])).astype(
            jnp.bfloat16
        )
        swap.wait()
        qb[:, pl.ds(mid, shared)] = qb[:, pl.ds(mid, shared)] + xrecv[step, 0]
        kb[:, pl.ds(mid, shared)] = kb[:, pl.ds(mid, shared)] + xrecv[step, 1]
        for k in range(1, n):
            src = lax.rem(me + k, n)
            remote(
                ssend.at[step],
                srecv.at[step, src],
                ssend_sems.at[step, k],
                srecv_sems.at[step, src],
                sibling,
            ).wait_recv()
        total = jnp.sum(srecv[step], axis=0)
        inv = lax.rsqrt(total * (1.0 / width) + 1e-06)
        q_col = jnp.transpose(jnp.broadcast_to(inv[0:1], (rows, rows)))[:, 0:1] * scale
        k_row = inv[1:2]
        for h in range(local // head):
            at = slice(h * head, (h + 1) * head)
            s = dot_nt(qb[:, at], kb[:, at]) * q_col * k_row
            s = jnp.where(allowed, s, -1e30)
            w = jnp.exp(s - jnp.max(s, axis=-1, keepdims=True))
            placed[:, at] = jnp.dot(
                w.astype(jnp.bfloat16), vb[:, at], preferred_element_type=jnp.float32
            ) / jnp.sum(w, axis=-1, keepdims=True)
        if step == 0:
            own_tk.wait()
            own_tv.wait()
            for k in range(1, n):
                src = lax.rem(me + k, n)
                for kind, d in enumerate((tk, tv)):
                    remote(
                        d.at[pl.ds(src * trows, trows)],
                        d.at[pl.ds(src * trows, trows)],
                        tsend_sems.at[kind, k],
                        trecv_sems.at[kind, src],
                        sibling,
                    ).wait_recv()
        parts = []
        for h in range(local // head):
            at = slice(h * head, (h + 1) * head)
            t = dot_nt(qb[:, at], tk[:, at]) * q_col
            w = jnp.exp(t - jnp.max(t, axis=-1, keepdims=True))
            b = jnp.dot(
                w.astype(jnp.bfloat16), tv[:, at], preferred_element_type=jnp.float32
            ) / jnp.sum(w, axis=-1, keepdims=True)
            parts.append(placed[:, at] + b)
        pack(
            jnp.where(mine, jnp.concatenate(parts, axis=1), 0.0), gathered.at[2 * step, me]
        )
        finish()
        finish = gather(block_view(2 * step), CHUNKS, 2 * step + 1)
        unpack(gathered.at[2 * step], full, 0, rows)
        if step == 0:
            loads[3].wait()
        projected = place(dot_nt(full[...], wo[...]))
        for s in range(n):
            placed[s * span : (s + 1) * span, :] = jnp.broadcast_to(
                mods[2, s : s + 1, pl.ds(start_col, local)], (span, local)
            )
        state = jnp.where(
            mine, current[:, pl.ds(start_col, local)] + placed[...] * projected, 0.0
        )
        if step < STEPS - 1:
            pack(state, gathered.at[2 * step + 1, me])
            finish()
            finish = gather(block_view(2 * step + 1), CHUNKS, 2 * step + 2)
        else:
            osend[...] = state.reshape(n, span, local).astype(jnp.bfloat16)
            for k in range(1, n):
                target = lax.rem(me + k, n)
                c = remote(
                    osend.at[target],
                    orecv.at[me],
                    osend_sems.at[k],
                    orecv_sems.at[me],
                    target,
                )
                c.start()
                pending.append(c)
            orecv[me] = osend[me]
    for k in range(1, n):
        src = lax.rem(me + k, n)
        remote(
            osend.at[src], orecv.at[src], osend_sems.at[k], orecv_sems.at[src], sibling
        ).wait_recv()
    assemble(orecv, out, 0, span)
    for c in text:
        c.wait_send()
    finish()
    drain()


def per_device_fused(
    hidden,
    incoming,
    levels,
    mod_table,
    query_weight,
    key_weight,
    value_weight,
    output_weight,
    query_gain,
    key_gain,
    text_keys,
    text_values,
):
    n = lax.axis_size("queue")
    span, width = hidden.shape
    cols = query_weight.shape[1]
    head = width // HEADS
    local = -(-cols // head) * head
    shared = 2 * local - 2 * cols
    step_off = 2 * cols - local
    rows = n * span
    text = n * text_keys.shape[0]
    vmem = pl.BlockSpec(memory_space=pltpu.VMEM)
    anywhere = pl.BlockSpec(memory_space=pl.ANY)
    dma = pltpu.SemaphoreType.DMA
    bf16, f32 = jnp.bfloat16, jnp.float32
    weight = pltpu.VMEM((cols, width), bf16)
    most = max(FIRST_CHUNKS, CHUNKS)
    return pl.pallas_call(
        functools.partial(fused_kernel, n, cols),
        out_shape=jax.ShapeDtypeStruct((span, width), hidden.dtype),
        in_specs=[anywhere, vmem, vmem] + [anywhere] * 5 + [vmem] * 2 + [anywhere] * 2,
        out_specs=vmem,
        scratch_shapes=[
            pltpu.VMEM((3, mod_table.shape[0], width), bf16),
            pltpu.VMEM((3, n, width), f32),
            weight,
            weight,
            weight,
            weight,
            pltpu.VMEM((n, span, width), bf16),
            pltpu.VMEM((2 * STEPS - 1, n, rows * cols // step_off, step_off), bf16),
            pltpu.VMEM((rows, width), f32),
            pltpu.VMEM((rows, width), bf16),
            pltpu.VMEM((rows, local), f32),
            pltpu.VMEM((rows, local), bf16),
            pltpu.VMEM((rows, local), bf16),
            pltpu.VMEM((rows, local), bf16),
            pltpu.VMEM((STEPS, 2, rows, shared), bf16),
            pltpu.VMEM((STEPS, 2, rows, shared), bf16),
            pltpu.VMEM((STEPS, 2, rows), f32),
            pltpu.VMEM((STEPS, n, 2, rows), f32),
            pltpu.VMEM((text, local), bf16),
            pltpu.VMEM((text, local), bf16),
            pltpu.VMEM((n, span, local), bf16),
            pltpu.VMEM((n, span, local), bf16),
            dma((8,)),
            dma((2, 4, n, most)),
            dma((2 * STEPS, n, most)),
            dma((STEPS, n)),
            dma((STEPS, n)),
            dma((STEPS,)),
            dma((STEPS,)),
            dma((2, n)),
            dma((2, n)),
            dma((n,)),
            dma((n,)),
        ],
        compiler_params=pltpu.CompilerParams(
            collective_id=0, has_side_effects=True, vmem_limit_bytes=60 * 1024 * 1024
        ),
    )(
        hidden,
        incoming,
        levels.reshape(1, n),
        mod_table.transpose(1, 0, 2),
        query_weight.T,
        key_weight.T,
        value_weight.T,
        output_weight.T,
        query_gain.reshape(1, width),
        key_gain.reshape(1, width),
        text_keys,
        text_values,
    )


def fits_fused(count, rows_total, width, groups):
    head = width // HEADS
    cols = width // count
    span = rows_total // (count * groups)
    return (
        count % 4 == 0
        and head == 128
        and span == 8
        and (2 * cols) % head == 0
        and cols % head == head // 2
        and cols > head
        and count * span == 128
    )


def choose(mesh):
    def run(hidden, incoming, levels, mod_table, *rest):
        count = lax.axis_size("queue")
        if fits_fused(count, hidden.shape[0] * count, hidden.shape[1], 1):
            return per_device_fused(hidden, incoming, levels, mod_table, *rest)
        return per_device(hidden, incoming, levels, mod_table, *rest)

    return run


def solution(mesh):
    in_specs = (
        P(("groups", "queue"), None),
        P(None, "groups", None),
        P(),
        P(),
        P(None, "queue"),
        P(None, "queue"),
        P(None, "queue"),
        P(None, "queue"),
        P(),
        P(),
        P(("groups", "queue"), None),
        P(("groups", "queue"), None),
    )
    out_specs = P(("groups", "queue"), None)
    return jax.shard_map(
        choose(mesh), mesh=mesh, in_specs=in_specs, out_specs=out_specs, check_vma=False
    )
```
